256 devices in a mesh: gx: 32 (over y, x, core), gy: 8 (over z).
Axes of the slice: x: 4, y: 4, z: 8, core: 2. Of those that a mesh axis runs over, the one named last changes fastest.
Arguments:
- labels: float32 [262144, 512], P(('gx', 'gy')), may hold values from -6 to 6
- point_order: int32 [256, 1024], P(('gx', 'gy')), may hold values from 0 to 1023, each once within a row
- leaf_inverse: float32 [262144, 1024], P(('gx', 'gy')), as said below
- leaf_basis: float32 [262144, 256], P(('gx', 'gy')), may hold values from -0.1875 to 0.1875
- couple_one: float32 [65536, 1024], P(('gx', 'gy'))
- transfer_one: float32 [65536, 256], P(('gx', 'gy')), may hold values from -0.1875 to 0.1875
- couple_two: float32 [16384, 1024], P(('gx', 'gy'))
- transfer_two: float32 [16384, 256], P(('gx', 'gy')), may hold values from -0.1875 to 0.1875
- couple_top: float32 [65536, 256], P(('gx', 'gy'))
Outputs:
- solution: float32 [262144, 512], P(('gx', 'gy'))
The draws below stay inside these ranges and needn't reach their ends.
Inputs may be any that keep to these rules, and one draw needn't show every extreme that they name: Each row of point_order is a permutation of 0 to 1023. leaf_inverse, couple_one, couple_two and the top matrix assembled from couple_top are dense with a dominant diagonal.
All inputs are finite; a program needn't handle non-finite values.
Results may differ from the reference program's by a relative error of at most 0.00011.
Values sent between devices are 32-bit elements; how exact they have to be, the bound alone decides.
No kernel may reach another device: no remote copies, remote signals or barrier semaphores. Data moves between devices by JAX's collectives and lax.ppermute only.
A program may use at most 64 MiB of HBM per device.

```python
import math
import jax
import jax.numpy as jnp
from jax import lax

LEAF = 1024
RANK = 256
COLS = 512
NLEAF = 256
NTOP = 16
POINTS = 262144


def dominant(key, height, breadth):
    key_diag, key_rest = jax.random.split(jax.random.fold_in(key, 7))
    diagonal = jnp.exp(jax.random.uniform(key_diag, (height, 1), jnp.float32, math.log(0.5), math.log(2.0)))
    spread_part = jax.random.normal(key_rest, (height, breadth), jnp.float32) * (0.5 / math.sqrt(breadth))
    row_pos = lax.broadcasted_iota(jnp.int32, (height, breadth), 0) % breadth
    col_pos = lax.broadcasted_iota(jnp.int32, (height, breadth), 1)
    return spread_part + jnp.where(row_pos == col_pos, diagonal, 0.0)


def draw_leaf_inverse(key, part):
    return dominant(key, NLEAF * LEAF, LEAF)


def draw_couple_one(key, part):
    return dominant(key, NLEAF * RANK, 4 * RANK)


def draw_couple_two(key, part):
    return dominant(key, NLEAF * RANK // 4, 4 * RANK)


def draw_couple_top(key, part):
    full_top = dominant(key, NTOP * RANK, NTOP * RANK)
    slice_rows = RANK // 16
    return full_top.reshape(NTOP, 16, slice_rows, NTOP, RANK).transpose(3, 1, 0, 2, 4).reshape(NTOP * NTOP * RANK, RANK)


def shard_levels(stream_key, dims, shards, low, top_value):
    def one(position, shards_of):
        heights = jax.random.uniform(jax.random.fold_in(jax.random.fold_in(stream_key, 6), position), (shards_of,), jnp.float32, low / len(shards), top_value / len(shards))
        return jnp.repeat(jnp.exp(heights), dims[position] // shards_of).reshape((-1,) + (1,) * (len(dims) - position - 1))

    gain = one(*shards[0])
    for cut in shards[1:]:
        gain = gain * one(*cut)
    return gain


def noise(stream_key, dims, deviation, most, cuts=(), dtype=jnp.bfloat16):
    drawn = deviation * jax.random.normal(stream_key, dims, jnp.float32)
    if cuts:
        drawn = drawn * shard_levels(stream_key, dims, cuts, -0.22, 0.18)
    return jnp.clip(drawn, -most, most).astype(dtype)


def setup_inputs(seed: int = 0) -> dict:
    key_list = jax.random.split(jax.random.key(seed), 10)
    labels = noise(key_list[0], (POINTS, COLS), 1.0, 6.0, ((0, 256),), jnp.float32)
    point_order = jax.vmap(lambda own: jax.random.permutation(own, LEAF))(jax.random.split(key_list[1], NLEAF)).reshape((NLEAF, LEAF)).astype(jnp.int32)
    leaf_inverse = draw_leaf_inverse(jax.random.fold_in(key_list[9], 71), 0)
    leaf_basis = noise(key_list[3], (POINTS, RANK), LEAF ** -0.5, 0.1875, ((0, 256),), jnp.float32)
    couple_one = draw_couple_one(jax.random.fold_in(key_list[9], 71), 0)
    transfer_one = noise(key_list[5], (NLEAF * RANK, RANK), (4 * RANK) ** -0.5, 0.1875, ((0, 256),), jnp.float32)
    couple_two = draw_couple_two(jax.random.fold_in(key_list[9], 71), 0)
    transfer_two = noise(key_list[7], (NLEAF * RANK // 4, RANK), (4 * RANK) ** -0.5, 0.1875, ((0, 256),), jnp.float32)
    couple_top = draw_couple_top(jax.random.fold_in(key_list[9], 71), 0)
    return {"labels": labels, "point_order": point_order, "leaf_inverse": leaf_inverse, "leaf_basis": leaf_basis, "couple_one": couple_one, "transfer_one": transfer_one, "couple_two": couple_two, "transfer_two": transfer_two, "couple_top": couple_top}


def batched(left, right):
    return jnp.einsum("nij,njc->nic", left, right, precision=lax.Precision.HIGHEST)


def batched_left(left, right):
    return jnp.einsum("nir,nic->nrc", left, right, precision=lax.Precision.HIGHEST)


def reference(labels, point_order, leaf_inverse, leaf_basis, couple_one, transfer_one, couple_two, transfer_two, couple_top):
    nodes_one = NLEAF // 4
    nodes_two = NLEAF // 16
    slice_rows = RANK // 16
    blocks = labels.reshape(NLEAF, LEAF, COLS)
    rhs = jax.vmap(lambda block, index: block[index])(blocks, point_order)
    inverse = leaf_inverse.reshape(NLEAF, LEAF, LEAF)
    basis = leaf_basis.reshape(NLEAF, LEAF, RANK)
    solved = batched(inverse, rhs)
    proj = batched_left(basis, solved)
    couple_a = couple_one.reshape(nodes_one, 4 * RANK, 4 * RANK)
    trans_a = transfer_one.reshape(nodes_one, 4 * RANK, RANK)
    solve_one = batched(couple_a, proj.reshape(nodes_one, 4 * RANK, COLS))
    reduced_one = batched_left(trans_a, solve_one)
    couple_b = couple_two.reshape(nodes_two, 4 * RANK, 4 * RANK)
    trans_b = transfer_two.reshape(nodes_two, 4 * RANK, RANK)
    solve_two = batched(couple_b, reduced_one.reshape(nodes_two, 4 * RANK, COLS))
    reduced_two = batched_left(trans_b, solve_two)
    full_top = couple_top.reshape(NTOP, 16, NTOP, slice_rows, RANK).transpose(2, 1, 3, 0, 4).reshape(NTOP * RANK, NTOP * RANK)
    solve_top = jnp.dot(full_top, reduced_two.reshape(NTOP * RANK, COLS), precision=lax.Precision.HIGHEST)
    block_two = solve_top.reshape(nodes_two, RANK, COLS)
    fixed_two = solve_two - batched(couple_b, batched(trans_b, block_two))
    block_one = fixed_two.reshape(nodes_one, RANK, COLS)
    fixed_one = solve_one - batched(couple_a, batched(trans_a, block_one))
    block_leaf = fixed_one.reshape(NLEAF, RANK, COLS)
    tree = solved - batched(inverse, batched(basis, block_leaf))
    placed = jax.vmap(lambda block, index: jnp.zeros_like(block).at[index].set(block))(tree, point_order)
    return placed.reshape(NLEAF * LEAF, COLS)
```

```python
import jax
import jax.numpy as jnp
from jax import lax
from jax.sharding import PartitionSpec as P

ALL = ("gx", "gy")


def dot(left, right, left_dim=1, right_dim=0):
    return lax.dot_general(
        left, right, (((left_dim,), (right_dim,)), ((), ())), precision=lax.Precision.HIGH
    )


def line_shift(value, step):
    pairs = [(i, i + step) for i in range(256) if 0 <= (i & 3) + step < 4]
    return lax.ppermute(value, ALL, pairs)


def ring_shift(value, step):
    return lax.ppermute(value, "gy", [(i, (i + step) % 8) for i in range(8)])


def other_core(value):
    return lax.ppermute(value, "gx", [(i, i ^ 1) for i in range(32)])


def node_exchange(pieces):
    groups = [[16 * g + i for i in range(16)] for g in range(16)]
    return lax.all_to_all(pieces, ALL, 0, 0, axis_index_groups=groups)


def line_gather(block):
    right, left = [block], [block]
    for _ in range(3):
        right.append(line_shift(right[-1], 1))
        left.append(line_shift(left[-1], -1))
    return [block] + [right[s] + left[4 - s] for s in (1, 2, 3)]


def node_gather(block, core):
    mine = lax.all_to_all(jnp.broadcast_to(block[None], (8,) + block.shape), "gy", 0, 0)
    theirs = other_core(mine)
    both = jnp.where(core == 0, jnp.stack([mine, theirs]), jnp.stack([theirs, mine]))
    return both.reshape((16 * block.shape[0], block.shape[1]))


def gather_rows(block, core, z):
    right, left = [block], [block]
    for _ in range(4):
        right.append(ring_shift(right[-1], 1))
    for _ in range(3):
        left.append(ring_shift(left[-1], -1))
    rows = block.shape[0]
    whole = jnp.zeros((16 * rows, block.shape[1]), block.dtype)
    for s in range(-3, 5):
        piece = right[s] if s >= 0 else left[-s]
        source = (z - s) & 7
        whole = lax.dynamic_update_slice(whole, piece, ((core * 8 + source) * rows, 0))
        whole = lax.dynamic_update_slice(
            whole, other_core(piece), (((1 - core) * 8 + source) * rows, 0)
        )
    return whole


def per_device(
    labels,
    point_order,
    leaf_inverse,
    leaf_basis,
    couple_one,
    transfer_one,
    couple_two,
    transfer_two,
    couple_top,
):
    gx, z = lax.axis_index("gx"), lax.axis_index("gy")
    core = gx & 1
    child = z & 3
    node = core * 2 + (z >> 2)
    order_row = point_order[0]

    transfers = line_gather(transfer_one)
    level_two = gather_rows(jnp.concatenate([couple_two, transfer_two], 1), core, z)
    couple_two_all, transfer_two_all = level_two[:, :1024], level_two[:, 1024:]

    rhs = labels[order_row]
    solved = dot(leaf_inverse, rhs)
    proj = dot(leaf_basis, solved, 0, 0)
    blocks = line_gather(proj)
    couples = [
        lax.dynamic_slice(couple_one, (0, ((child - s) & 3) * 256), (256, 256)) for s in range(4)
    ]
    couple_turned = jnp.concatenate(couples, 1)

    back = dot(leaf_inverse, leaf_basis)
    unorder = lambda rows: jnp.zeros_like(rows).at[order_row].set(rows, unique_indices=True)
    back_out = unorder(back)
    solved_out = unorder(solved)
    lift_one = dot(couple_turned, jnp.concatenate(transfers, 0))
    couple_two_own = lax.dynamic_slice(couple_two_all, (node * 256, 0), (256, 1024))
    lift_two = dot(couple_two_own, transfer_two_all)
    lift_both = dot(lift_one, lift_two)
    top_out = dot(back_out, lift_both)

    solve_one = dot(couple_turned, jnp.concatenate(blocks, 0))
    partial = dot(solve_one, transfer_one, 0, 0)
    parts = node_exchange(partial.reshape(16, 32, 256))
    stack_two = parts.reshape(4, 4, 32, 256).sum(1)
    stack_two = jnp.concatenate([stack_two[c] for c in range(4)], 1)
    solve_two = dot(stack_two, couple_two_all, 1, 1)
    reduced_two = dot(solve_two, transfer_two_all)
    send = jnp.stack(
        [
            jnp.concatenate([solve_two[:, (q >> 2) * 256 : (q >> 2) * 256 + 256], reduced_two], 0)
            for q in range(16)
        ]
    )
    got = node_exchange(send)
    solve_two_own = got[:, :32].reshape(512, 256)
    reduced_all = got[:, 32:].reshape(512, 256)

    top_partial = dot(couple_top, reduced_all, 1, 1).reshape(16, 16, 512)
    planes = [[i for i in range(32) if i % 2 == k] for k in range(2)]
    own_rows = lax.all_to_all(top_partial, "gx", 0, 0, axis_index_groups=planes).sum(0)
    block_two = node_gather(own_rows, core)

    known = solve_one - dot(lift_one, solve_two_own, 1, 1)
    base_out = solved_out - dot(back_out, known)
    return base_out - dot(top_out, block_two)


def solution(mesh):
    spec = P(ALL, None)
    return jax.shard_map(
        per_device, mesh=mesh, in_specs=(spec,) * 9, out_specs=spec, check_vma=False
    )
```

```python
import jax
import jax.numpy as jnp
from jax import lax
from jax.experimental import pallas as pl
from jax.experimental.pallas import tpu as pltpu
from jax.sharding import PartitionSpec as P


ALL = ("gx", "gy")


def dot(left, right, left_dim=1, right_dim=0):
    return lax.dot_general(
        left, right, (((left_dim,), (right_dim,)), ((), ())), precision=lax.Precision.HIGH
    )


def line_shift(value, step, senders):
    pairs = [(i, i + step) for i in range(256) if i & 3 in senders]
    return lax.ppermute(value, ALL, pairs)


def ring_shift(value, step):
    return lax.ppermute(value, "gy", [(i, (i + step) % 8) for i in range(8)])


def other_core(value):
    return lax.ppermute(value, "gx", [(i, i ^ 1) for i in range(32)])


def join_partner(value, z, bit):
    other = lax.ppermute(value, "gy", [(i, i ^ 1 << bit) for i in range(8)])
    return jnp.where(z >> bit & 1 == 0, jnp.stack([value, other]), jnp.stack([other, value]))


def node_exchange(pieces):
    groups = [[16 * g + i for i in range(16)] for g in range(16)]
    return lax.all_to_all(pieces, ALL, 0, 0, axis_index_groups=groups)


def column(matrix, index):
    return lax.dynamic_slice(matrix, (0, (index & 3) * 256), (256, 256))


def node_gather(block, core):
    mine = lax.all_to_all(jnp.broadcast_to(block[None], (8,) + block.shape), "gy", 0, 0)
    theirs = other_core(mine)
    both = jnp.where(core == 0, jnp.stack([mine, theirs]), jnp.stack([theirs, mine]))
    return both.reshape((16 * block.shape[0], block.shape[1]))


def place_kernel(z_ref, *refs):
    pieces, (couple_ref, transfer_ref) = refs[:8], refs[8:]
    for k, s in enumerate(range(-3, 5)):
        row = pl.multiple_of(((z_ref[0] - s) & 7) * 64, 64)
        couple_ref[pl.ds(row, 64), :] = pieces[k][:, :1024]
        transfer_ref[pl.ds(row, 64), :] = pieces[k][:, 1024:]


def place_rows(pieces, z):
    return pl.pallas_call(
        place_kernel,
        out_shape=(
            jax.ShapeDtypeStruct((512, 1024), jnp.float32),
            jax.ShapeDtypeStruct((512, 256), jnp.float32),
        ),
        in_specs=[pl.BlockSpec(memory_space=pltpu.SMEM)]
        + [pl.BlockSpec(memory_space=pltpu.VMEM)] * 8,
        out_specs=(pl.BlockSpec(memory_space=pltpu.VMEM),) * 2,
    )(z.reshape(1), *pieces)


def per_device(
    labels,
    point_order,
    leaf_inverse,
    leaf_basis,
    couple_one,
    transfer_one,
    couple_two,
    transfer_two,
    couple_top,
):
    gx, z = lax.axis_index("gx"), lax.axis_index("gy")
    core, child, half = gx & 1, z & 3, z >> 2
    order_row = point_order[0]
    barrier = lax.optimization_barrier

    unorder = lambda rows: jnp.zeros_like(rows).at[order_row].set(rows, unique_indices=True)

    gains = dot(transfer_one, couple_one, 0, 0)
    ring = jnp.concatenate([couple_two, transfer_two], 1)
    gain_right = line_shift(column(gains, child + 3), 1, (0,))
    gain_left = line_shift(column(gains, child - 3), -1, (3,))
    ring_right, ring_left = ring_shift(ring, 1), ring_shift(ring, -1)
    rhs = labels[order_row]
    gain_right, gain_left, ring_right, ring_left, rhs = barrier(
        (gain_right, gain_left, ring_right, ring_left, rhs)
    )
    rings = {0: ring, 1: ring_right, -1: ring_left}

    gain_right = line_shift(column(gains, child + 2) + gain_right, 1, (0, 1))
    gain_left = line_shift(column(gains, child - 2) + gain_left, -1, (3, 2))
    ring_right, ring_left = ring_shift(ring_right, 1), ring_shift(ring_left, -1)
    solved = dot(leaf_inverse, rhs)
    gain_right, gain_left, ring_right, ring_left, solved = barrier(
        (gain_right, gain_left, ring_right, ring_left, solved)
    )
    rings |= {2: ring_right, -2: ring_left}

    gain_right = line_shift(column(gains, child + 1) + gain_right, 1, (0, 1, 2))
    gain_left = line_shift(column(gains, child - 1) + gain_left, -1, (3, 2, 1))
    ring_right, ring_left = ring_shift(ring_right, 1), ring_shift(ring_left, -1)
    proj = dot(leaf_basis, solved, 0, 0)
    block = jnp.concatenate([proj, transfer_one], 1)
    gain_right, gain_left, ring_right, ring_left, proj, block, leaf_inverse = barrier(
        (gain_right, gain_left, ring_right, ring_left, proj, block, leaf_inverse)
    )
    rings |= {3: ring_right, -3: ring_left}

    ring_right = ring_shift(ring_right, 1)
    gain_one = column(gains, child) + gain_right + gain_left
    partial = dot(proj, gain_one, 0, 1)
    parts = node_exchange(partial.reshape(16, 32, 256))
    right_one = line_shift(block, 1, (0, 1, 2))
    left_one = line_shift(block, -1, (3, 2, 1))
    back = dot(leaf_inverse, leaf_basis)
    back_out = unorder(back)
    solved_out = unorder(solved)
    parts, ring_right, right_one, left_one, back_out, solved_out = barrier(
        (parts, ring_right, right_one, left_one, back_out, solved_out)
    )
    rings |= {4: ring_right}

    right_two = line_shift(right_one, 1, (1, 2))
    left_two = line_shift(left_one, -1, (2, 1))
    couple_core, transfer_core = place_rows([rings[s] for s in range(-3, 5)], z)
    stack_mine = parts.reshape(4, 4, 32, 256).sum(1)
    stack_other = other_core(stack_mine)
    stack_two = jnp.where(
        core == 0,
        jnp.concatenate([stack_mine, stack_other], 1),
        jnp.concatenate([stack_other, stack_mine], 1),
    )
    stack_two = jnp.concatenate([stack_two[c] for c in range(4)], 1)
    solve_two = dot(stack_two, couple_core, 1, 1)
    far = lax.ppermute(
        jnp.where(half == 0, solve_two[:, 256:], solve_two[:, :256]),
        "gy",
        [(i, i ^ 4) for i in range(8)],
    )
    near = jnp.where(half == 0, solve_two[:, :256], solve_two[:, 256:])
    shares = jnp.where(half == 0, jnp.stack([near, far]), jnp.stack([far, near]))
    reduced = dot(solve_two, transfer_core)
    reduced = lax.dynamic_slice(reduced, (core * 32, 0), (32, 256)) + other_core(
        lax.dynamic_slice(reduced, ((1 - core) * 32, 0), (32, 256))
    )
    reduced_all = node_gather(reduced, core)
    reduced_all, right_two, left_two, shares = barrier((reduced_all, right_two, left_two, shares))

    right_three = line_shift(right_two, 1, (2,))
    left_three = line_shift(left_two, -1, (1,))
    shares = join_partner(shares, z, 0)
    top_partial = dot(couple_top, reduced_all, 1, 1).reshape(16, 16, 512)
    planes = [[i for i in range(32) if i % 2 == k] for k in range(2)]
    own_rows = lax.all_to_all(top_partial, "gx", 0, 0, axis_index_groups=planes).sum(0)
    own_rows, right_three, left_three, shares = barrier(
        (own_rows, right_three, left_three, shares)
    )

    shares = join_partner(shares, z, 1)
    block_two = node_gather(own_rows, core)

    couple_turned = jnp.concatenate([column(couple_one, child - s) for s in range(4)], 1)
    stack_one = jnp.concatenate(
        [block, right_one + left_three, right_two + left_two, right_three + left_one], 0
    )
    solve_lift = dot(couple_turned, stack_one)
    solve_one, lift_one = solve_lift[:, :512], solve_lift[:, 512:]

    transfer_other = other_core(transfer_core)
    transfer_all = jnp.where(
        core == 0,
        jnp.concatenate([transfer_core, transfer_other], 0),
        jnp.concatenate([transfer_other, transfer_core], 0),
    )
    lift_two = dot(lax.dynamic_slice(couple_core, (half * 256, 0), (256, 1024)), transfer_all)
    lift_both = dot(lift_one, lift_two)
    top_out = dot(back_out, lift_both)
    shares = shares.reshape(2, 2, 2, 2, 32, 256).transpose(3, 2, 0, 1, 4, 5)
    solve_two_own = shares.reshape(512, 256)
    known = solve_one - dot(lift_one, solve_two_own, 1, 1)
    base_out = solved_out - dot(back_out, known)
    return base_out - dot(top_out, block_two)


def solution(mesh):
    spec = P(ALL, None)
    return jax.shard_map(per_device, mesh=mesh, in_specs=(spec,) * 9, out_specs=spec, check_vma=False)
```

```python
import jax
import jax.numpy as jnp
from jax import lax
from jax.experimental import pallas as pl
from jax.experimental.pallas import tpu as pltpu
from jax.sharding import PartitionSpec as P


ALL = ("gx", "gy")


def dot(left, right, left_dim=1, right_dim=0):
    return lax.dot_general(
        left, right, (((left_dim,), (right_dim,)), ((), ())), precision=lax.Precision.HIGH
    )


def line_shift(value, step, senders):
    pairs = [(i, i + step) for i in range(256) if i & 3 in senders]
    return lax.ppermute(value, ALL, pairs)


def ring_shift(value, step):
    return lax.ppermute(value, "gy", [(i, (i + step) % 8) for i in range(8)])


def other_core(value):
    return lax.ppermute(value, "gx", [(i, i ^ 1) for i in range(32)])


def node_exchange(pieces):
    groups = [[16 * g + i for i in range(16)] for g in range(16)]
    return lax.all_to_all(pieces, ALL, 0, 0, axis_index_groups=groups)


def column(matrix, index):
    return lax.dynamic_slice(matrix, (0, (index & 3) * 256), (256, 256))


def node_gather(block, core):
    mine = lax.all_to_all(jnp.broadcast_to(block[None], (8,) + block.shape), "gy", 0, 0)
    theirs = other_core(mine)
    both = jnp.where(core == 0, jnp.stack([mine, theirs]), jnp.stack([theirs, mine]))
    return both.reshape((16 * block.shape[0], block.shape[1]))


def place_kernel(z_ref, *refs):
    pieces, (couple_ref, transfer_ref) = refs[:8], refs[8:]
    for k, s in enumerate(range(-3, 5)):
        row = pl.multiple_of(((z_ref[0] - s) & 7) * 64, 64)
        couple_ref[pl.ds(row, 64), :] = pieces[k][:, :1024]
        transfer_ref[pl.ds(row, 64), :] = pieces[k][:, 1024:]


def place_rows(pieces, z):
    return pl.pallas_call(
        place_kernel,
        out_shape=(
            jax.ShapeDtypeStruct((512, 1024), jnp.float32),
            jax.ShapeDtypeStruct((512, 256), jnp.float32),
        ),
        in_specs=[pl.BlockSpec(memory_space=pltpu.SMEM)]
        + [pl.BlockSpec(memory_space=pltpu.VMEM)] * 8,
        out_specs=(pl.BlockSpec(memory_space=pltpu.VMEM),) * 2,
    )(z.reshape(1), *pieces)


def inverse(order):
    count = order.shape[0]
    place = lax.broadcasted_iota(jnp.int32, (count, count), 1)
    found = order[None, :] == lax.broadcasted_iota(jnp.int32, (count, count), 0)
    return jnp.sum(jnp.where(found, place, 0), 1)


def per_device(
    labels,
    point_order,
    leaf_inverse,
    leaf_basis,
    couple_one,
    transfer_one,
    couple_two,
    transfer_two,
    couple_top,
):
    gx, z = lax.axis_index("gx"), lax.axis_index("gy")
    core, child, half = gx & 1, z & 3, z >> 2
    order_row = point_order[0]
    barrier = lax.optimization_barrier

    gains = dot(transfer_one, couple_one, 0, 0)
    ring = jnp.concatenate([couple_two, transfer_two], 1)
    pairs = [(i, i + (1 if i & 3 == 0 else -1)) for i in range(256) if i & 3 in (0, 3)]
    gain = lax.ppermute(column(gains, jnp.where(child == 0, 3, 0)), ALL, pairs)
    ring_right, ring_left = ring_shift(ring, 1), ring_shift(ring, -1)
    rhs = labels[order_row]
    inverse_order = inverse(order_row)
    gain, ring_right, ring_left, rhs, inverse_order = barrier(
        (gain, ring_right, ring_left, rhs, inverse_order)
    )
    gain_right, gain_left = (jnp.where(child == 1, gain, 0.0), jnp.where(child == 2, gain, 0.0))
    rings = {0: ring, 1: ring_right, -1: ring_left}

    gain_right = line_shift(column(gains, child + 2) + gain_right, 1, (0, 1))
    gain_left = line_shift(column(gains, child - 2) + gain_left, -1, (3, 2))
    ring_right, ring_left = ring_shift(ring_right, 1), ring_shift(ring_left, -1)
    solved = dot(leaf_inverse, rhs)
    gain_right, gain_left, ring_right, ring_left, solved = barrier(
        (gain_right, gain_left, ring_right, ring_left, solved)
    )
    rings |= {2: ring_right, -2: ring_left}

    gain_right = line_shift(column(gains, child + 1) + gain_right, 1, (0, 1, 2))
    gain_left = line_shift(column(gains, child - 1) + gain_left, -1, (3, 2, 1))
    ring_right, ring_left = ring_shift(ring_right, 1), ring_shift(ring_left, -1)
    proj = dot(leaf_basis, solved, 0, 0)
    block = jnp.concatenate([proj, transfer_one], 1)
    gain_right, gain_left, ring_right, ring_left, proj, block, leaf_inverse = barrier(
        (gain_right, gain_left, ring_right, ring_left, proj, block, leaf_inverse)
    )
    rings |= {3: ring_right, -3: ring_left}

    ring_right = ring_shift(ring_right, 1)
    partial = dot(proj, column(gains, child) + gain_right + gain_left, 0, 1)
    parts = node_exchange(partial.reshape(16, 32, 256))
    right_one = line_shift(block, 1, (0, 1, 2))
    left_one = line_shift(block, -1, (3, 2, 1))
    back = dot(leaf_inverse, leaf_basis)
    rings |= {4: ring_right}
    couple_core, transfer_core = place_rows([rings[s] for s in range(-3, 5)], z)

    stack_mine = parts.reshape(4, 4, 32, 256).sum(1)
    stack_other = other_core(stack_mine)
    stack_two = jnp.where(
        core == 0,
        jnp.concatenate([stack_mine, stack_other], 1),
        jnp.concatenate([stack_other, stack_mine], 1),
    )
    stack_two = jnp.concatenate([stack_two[c] for c in range(4)], 1)
    solve_two = dot(stack_two, couple_core, 1, 1)
    reduced = dot(solve_two, transfer_core)
    reduced = lax.dynamic_slice(reduced, (core * 32, 0), (32, 256)) + other_core(
        lax.dynamic_slice(reduced, ((1 - core) * 32, 0), (32, 256))
    )
    reduced_all = node_gather(reduced, core)
    far = lax.ppermute(
        jnp.where(half == 0, solve_two[:, 256:], solve_two[:, :256]),
        "gy",
        [(i, i ^ 4) for i in range(8)],
    )
    right_two = line_shift(right_one, 1, (1, 2))
    left_two = line_shift(left_one, -1, (2, 1))
    back_out = back[inverse_order]
    transfer_other = other_core(transfer_core)
    transfer_all = jnp.where(
        core == 0,
        jnp.concatenate([transfer_core, transfer_other], 0),
        jnp.concatenate([transfer_other, transfer_core], 0),
    )
    lift_two = dot(lax.dynamic_slice(couple_core, (half * 256, 0), (256, 1024)), transfer_all)

    top_partial = dot(couple_top, reduced_all, 1, 1).reshape(16, 16, 512)
    planes = [[i for i in range(32) if i % 2 == k] for k in range(2)]
    own_rows = lax.all_to_all(top_partial, "gx", 0, 0, axis_index_groups=planes)
    near = jnp.where(half == 0, solve_two[:, :256], solve_two[:, 256:])
    shares = jnp.where(half == 0, jnp.stack([near, far]), jnp.stack([far, near]))
    far = lax.ppermute(shares, "gy", [(i, i ^ 2) for i in range(8)])
    right_three = line_shift(right_two, 1, (2,))
    left_three = line_shift(left_two, -1, (1,))
    solved_out = solved[inverse_order]
    couple_turned = jnp.concatenate([column(couple_one, child - s) for s in range(4)], 1)

    block_two = node_gather(own_rows.sum(0), core)
    shares = jnp.where(z & 2 == 0, jnp.stack([shares, far]), jnp.stack([far, shares]))
    far = lax.ppermute(shares, "gy", [(i, i ^ 1) for i in range(8)])

    stack_one = jnp.concatenate(
        [block, right_one + left_three, right_two + left_two, right_three + left_one], 0
    )
    solve_lift = dot(couple_turned, stack_one)
    solve_one, lift_one = solve_lift[:, :512], solve_lift[:, 512:]
    lift_both = dot(lift_one, lift_two)
    top_out = dot(back_out, lift_both)
    shares = jnp.where(z & 1 == 0, jnp.stack([shares, far]), jnp.stack([far, shares]))
    shares = shares.reshape(2, 2, 2, 2, 32, 256).transpose(3, 2, 1, 0, 4, 5)
    solve_two_own = shares.reshape(512, 256)
    known = solve_one - dot(lift_one, solve_two_own, 1, 1)
    both_out = jnp.concatenate([back_out, top_out], 1)
    return solved_out - dot(both_out, jnp.concatenate([known, block_two], 0))


def solution(mesh):
    spec = P(ALL, None)
    return jax.shard_map(per_device, mesh=mesh, in_specs=(spec,) * 9, out_specs=spec, check_vma=False)
```
